32 devices in a mesh: query: 4 (over x, core), db: 8 (over z, y).
Axes of the slice: x: 2, y: 2, z: 4, core: 2. Of those that a mesh axis runs over, the one named last changes fastest.
Arguments:
- logits: bfloat16 [20, 1048576], P(None, ('query', 'db')), may hold values from -40 to 340
- entry_ids: int32 [1048576], P(('query', 'db')), may hold values from 0 to 8191, as said below
- query_counts: bfloat16 [4096, 2400], P(('query', 'db')), may hold values from 0.0099 to 1
- idf_weights: float32 [2400], replicated, may hold values from 0.05 to 5
Outputs:
- block_max: float32 [16, 4096], P('db', 'query')
The draws below stay inside these ranges and needn't reach their ends.
Inputs may be any that keep to these rules, and one draw needn't show every extreme that they name: `entry_ids`: never falling; every entry 0 to 8191 has 32 or more residues, and some entry exactly 32. Shard s = q * 8 + d holds residues s * 32768 to (s + 1) * 32768 - 1, and no entry crosses a shard's edge. The shards of query index q together hold entries q * 2048 to (q + 1) * 2048 - 1; a shard holds at most 448 entries, and in every query index some shard holds exactly 448.
All inputs are finite; a program needn't handle non-finite values.
Results may differ from the reference program's by a relative error of at most 0.00074.
Values may be sent and summed in bfloat16 or wider, within the bound.
A program may use at most 64 MiB of HBM per device.

```python
import math
import jax
import jax.numpy as jnp
from jax import lax

STATES = 20
OFFSETS = 6
FEAT = 2400
R_DEV = 32768
LMIN = 32
BR = 256
BLOCK = 512
E_Q = 256
KMAX = 448
E_ROW = 2048
ENTRIES = 8192
RESIDUES = 1048576
QUERIES = 4096
NBLK = 16
N_QUERY = 4
N_DB = 8


def shuffled(seed_key):
    return jax.random.permutation(seed_key, N_DB)


def entry_layout(key):
    shards = N_QUERY * N_DB
    half_count = N_DB // 2
    swing_top = 3 * E_Q // 4
    perm_keys = jax.random.split(jax.random.fold_in(key, 101), N_QUERY)
    orders = jax.vmap(shuffled)(perm_keys)
    swings = jax.random.randint(jax.random.fold_in(key, 102), (N_QUERY, half_count), 0, swing_top + 1)
    swings = swings.at[:, 0].set(swing_top)
    values = jnp.concatenate([E_Q + swings, E_Q - swings], axis=1).astype(jnp.int32)
    row_index = jnp.broadcast_to(jnp.arange(N_QUERY, dtype=jnp.int32)[:, None], (N_QUERY, N_DB))
    shard_counts = jnp.zeros((N_QUERY, N_DB), jnp.int32).at[row_index, orders].set(values)
    entry_base = (jnp.arange(N_QUERY, dtype=jnp.int32) * E_ROW)[:, None] + jnp.cumsum(shard_counts, axis=1) - shard_counts
    shard_counts = shard_counts.reshape(shards)
    entry_base = entry_base.reshape(shards)
    weights = jax.random.randint(jax.random.fold_in(key, 103), (shards, KMAX), 1, 32).astype(jnp.int32)
    weights = weights.at[orders[0, 0], 0].set(0)
    position = jnp.arange(KMAX, dtype=jnp.int32)
    living = position[None, :] < shard_counts[:, None]
    weights = jnp.where(living, weights, 0)
    running = jnp.cumsum(weights, axis=1)
    weight_sum = running[:, -1]
    spare = R_DEV - shard_counts * LMIN
    before = running - weights
    starts = position[None, :] * LMIN + spare[:, None] * before // weight_sum[:, None]
    shard_axis = jnp.broadcast_to(jnp.arange(shards, dtype=jnp.int32)[:, None], (shards, KMAX))
    places = jnp.where(living & (position[None, :] >= 1), starts, R_DEV)
    boundary = jnp.zeros((shards, R_DEV + 1), jnp.int32).at[shard_axis, places].add(1)
    local_ids = jnp.cumsum(boundary[:, :R_DEV], axis=1)
    return (entry_base[:, None] + local_ids).reshape(shards * R_DEV).astype(jnp.int32)


def draw_entry_ids(key, part):
    return entry_layout(key)


def draw_logits(key, part):
    entry_of = entry_layout(key)
    leaning = jax.random.normal(jax.random.fold_in(key, 201), (STATES, ENTRIES), jnp.float32)
    jitter = jax.random.normal(jax.random.fold_in(key, 202), (STATES, RESIDUES), jnp.float32)
    values = jnp.clip(2.5 * jnp.take(leaning, entry_of, axis=1) + 2.0 * jitter, -40.0, 40.0)
    return values.astype(jnp.bfloat16)


def draw_query_counts(key, part):
    level_draw = jax.random.uniform(jax.random.fold_in(key, 301), (QUERIES, STATES), jnp.float32)
    state_level = level_draw ** 0.5
    noise_draw = jax.random.uniform(jax.random.fold_in(key, 302), (QUERIES, STATES, OFFSETS, STATES), jnp.float32)
    exponent = 2.0 * state_level[:, :, None, None] + 2.0 * state_level[:, None, None, :] + 0.6 * noise_draw
    return jnp.exp(-exponent).reshape(QUERIES, FEAT).astype(jnp.bfloat16)


def setup_inputs(seed: int = 0) -> dict:
    seeds = jax.random.split(jax.random.key(seed), 5)
    logits = draw_logits(jax.random.fold_in(seeds[4], 71), 0)
    entry_ids = draw_entry_ids(jax.random.fold_in(seeds[4], 71), 0)
    query_counts = draw_query_counts(jax.random.fold_in(seeds[4], 71), 0)
    idf_weights = jnp.clip(jnp.exp(jax.random.uniform(seeds[3], (FEAT,), jnp.float32, math.log(0.05), math.log(5.0))), 0.05, 5.0)
    return dict(logits=logits, entry_ids=entry_ids, query_counts=query_counts, idf_weights=idf_weights)


EPSILON = 1e-06

def normalized(counts, idf_weights):
    scaled = counts.astype(jnp.float32) * idf_weights
    return (scaled / jnp.sqrt(lax.optimization_barrier(jnp.sum(scaled * scaled, axis=-1, keepdims=True)) + EPSILON)).astype(jnp.bfloat16)

def shard_counts(logit_shard, id_shard):
    window = BR // LMIN + 1
    state_probs = jax.nn.softmax(logit_shard.astype(jnp.float32), axis=0).astype(jnp.bfloat16)
    local_ids = (id_shard - id_shard[0]).astype(jnp.int32)
    residues = local_ids.shape[0]
    padded = jnp.pad(state_probs, ((0, 0), (0, OFFSETS)))
    padded_ids = jnp.pad(local_ids, (0, OFFSETS), constant_values=-1)
    shifted = []
    for offset in range(OFFSETS):
        same_entry = padded_ids[offset + 1:offset + 1 + residues] == local_ids
        shifted.append(jnp.where(same_entry[None, :], padded[:, offset + 1:offset + 1 + residues], jnp.zeros((), jnp.bfloat16)))
    blocks = residues // BR
    partner = jnp.concatenate(shifted, axis=0).reshape(OFFSETS * STATES, blocks, BR)
    block_ids = local_ids.reshape(blocks, BR)
    starts = block_ids[:, 0]
    relative = block_ids - starts[:, None]
    columns = jnp.arange(window, dtype=jnp.int32)
    onehot = relative[:, None, :] == columns[None, :, None]
    probs_blocks = state_probs.reshape(STATES, blocks, BR).transpose(1, 0, 2)
    spread = jnp.where(onehot[:, :, None, :], probs_blocks[:, None, :, :], jnp.zeros((), jnp.bfloat16))
    spread = spread.reshape(blocks, window * STATES, BR)
    pair_sums = jnp.einsum('nkr,cnr->nkc', spread.astype(jnp.float32), partner.astype(jnp.float32), precision=lax.Precision.HIGHEST)
    targets = (starts[:, None] + columns[None, :]).reshape(-1).astype(jnp.int32)
    counts_table = jnp.zeros((KMAX + window, FEAT), jnp.float32).at[targets].add(pair_sums.reshape(-1, FEAT))
    return counts_table[:KMAX]

def reference(logits, entry_ids, query_counts, idf_weights):
    shards = N_QUERY * N_DB
    logit_shards = logits.reshape(STATES, shards, R_DEV).transpose(1, 0, 2)
    id_shards = entry_ids.reshape(shards, R_DEV)

    def encode_shard(pair):
        return normalized(shard_counts(pair[0], pair[1]), idf_weights)
    tables = lax.map(encode_shard, (logit_shards, id_shards))
    firsts = id_shards[:, 0]
    totals = id_shards[:, -1] - firsts + 1
    position = jnp.arange(KMAX, dtype=jnp.int32)
    target = jnp.where(position[None, :] < totals[:, None], firsts[:, None] + position[None, :], ENTRIES).astype(jnp.int32)
    entry_rows = jnp.zeros((ENTRIES + 1, FEAT), jnp.bfloat16).at[target.reshape(-1)].set(tables.reshape(-1, FEAT))[:ENTRIES]
    owned_rows = entry_rows.reshape(N_QUERY, E_Q, N_DB, FEAT).transpose(2, 0, 1, 3).reshape(ENTRIES, FEAT)
    queries = normalized(query_counts, idf_weights)

    def block_best(row_block):
        scores = jnp.dot(row_block, queries.T, preferred_element_type=jnp.float32)
        return lax.optimization_barrier(jnp.max(scores, axis=0))
    return lax.map(block_best, owned_rows.reshape(NBLK, BLOCK, FEAT))
```

```python
import functools

import jax
import jax.numpy as jnp
from jax import lax
from jax.experimental import pallas as pl
from jax.experimental.pallas import tpu as pltpu
from jax.sharding import PartitionSpec as P

STATES = 20
OFFSETS = 6
COLS = STATES * OFFSETS
LANES = 128
BR = 256
WINDOW = 16
E_DEV = 1024
HALVES = 2
CORES = 2
EPSILON = 1e-06
HALO = 128


def align_up(value, unit):
    return -(-value // unit) * unit


def encode_kernel(
    residues, rows, chunk, starts_ref, logits_ref, ids_ref, idf_ref, out_ref, probs, partner, table
):
    table[...] = jnp.zeros_like(table)
    partner[COLS:, :] = jnp.zeros((LANES - COLS, chunk), jnp.float32)
    probs[:, residues:] = jnp.zeros((STATES, HALO), jnp.float32)

    def soften(step, carry):
        cols = pl.ds(pl.multiple_of(step * chunk, chunk), chunk)
        values = logits_ref[:, cols].astype(jnp.float32)
        values = jnp.exp(values - jnp.max(values, axis=0, keepdims=True))
        values = values / jnp.sum(values, axis=0, keepdims=True)
        probs[:, cols] = values.astype(jnp.bfloat16).astype(jnp.float32)
        return carry

    lax.fori_loop(0, residues // chunk, soften, 0)
    slots = lax.broadcasted_iota(jnp.int32, (WINDOW, BR), 0)

    def add_chunk(step, carry):
        first = pl.multiple_of(step * chunk, chunk)
        wide = pl.ds(first, chunk + HALO)
        prob_slab = probs[:, wide]
        id_slab = ids_ref[:, wide]
        own_ids = id_slab[:, :chunk]
        for offset in range(OFFSETS):
            shift = chunk + HALO - offset - 1
            moved = pltpu.roll(prob_slab, shift, 1)[:, :chunk]
            moved_ids = pltpu.roll(id_slab, shift, 1)[:, :chunk]
            partner[offset * STATES : (offset + 1) * STATES, :] = jnp.where(
                moved_ids == own_ids, moved, 0.0
            )
        for block in range(chunk // BR):
            here = slice(block * BR, (block + 1) * BR)
            base = pl.multiple_of(starts_ref[step * (chunk // BR) + block], 8)
            onehot = (own_ids[:, here] - base) == slots
            spread = jnp.concatenate(
                [
                    jnp.where(onehot, prob_slab[a : a + 1, here], 0.0).astype(jnp.bfloat16)
                    for a in range(STATES)
                ],
                axis=0,
            )
            sums = lax.dot_general(
                spread,
                partner[:, here].astype(jnp.bfloat16),
                (((1,), (1,)), ((), ())),
                preferred_element_type=jnp.float32,
            )
            for a in range(STATES):
                table[a, pl.ds(base, WINDOW), :] += sums[a * WINDOW : (a + 1) * WINDOW]
        return carry

    lax.fori_loop(0, residues // chunk, add_chunk, 0)

    def finish(step, carry):
        part = pl.ds(pl.multiple_of(step * 16, 16), 16)
        total = jnp.zeros((16, LANES), jnp.float32)
        for a in range(STATES):
            scaled = table[a, part, :] * idf_ref[a : a + 1, :]
            total += scaled * scaled
        norm = jnp.sqrt(jnp.sum(total, axis=1, keepdims=True) + EPSILON)
        for a in range(STATES):
            scaled = table[a, part, :] * idf_ref[a : a + 1, :]
            out_ref[part, a * LANES : (a + 1) * LANES] = (scaled / norm).astype(jnp.bfloat16)
        return carry

    lax.fori_loop(0, rows // 16, finish, 0)


def encode(logits, entry_ids, idf_pad, rows, db_count):
    residues = logits.shape[1]
    chunk = min(2048, residues)
    first = entry_ids[0]
    local_ids = entry_ids - (first - lax.rem(first, db_count))
    starts = jnp.clip(local_ids[::BR] // 8 * 8, 0, rows - WINDOW)
    padded_ids = jnp.pad(local_ids, (0, HALO), constant_values=-1)[None, :]
    vmem = pl.BlockSpec(memory_space=pltpu.VMEM)
    return pl.pallas_call(
        functools.partial(encode_kernel, residues, rows, chunk),
        out_shape=jax.ShapeDtypeStruct((rows, STATES * LANES), jnp.bfloat16),
        in_specs=[pl.BlockSpec(memory_space=pltpu.SMEM), vmem, vmem, vmem],
        out_specs=vmem,
        scratch_shapes=[
            pltpu.VMEM((STATES, residues + HALO), jnp.float32),
            pltpu.VMEM((LANES, chunk), jnp.float32),
            pltpu.VMEM((STATES, rows, LANES), jnp.float32),
        ],
        cost_estimate=pl.CostEstimate(
            flops=2 * residues * STATES * WINDOW * LANES,
            bytes_accessed=residues * 44 + rows * STATES * LANES * 2,
            transcendentals=residues * STATES,
        ),
        compiler_params=pltpu.CompilerParams(vmem_limit_bytes=32 * 1024 * 1024),
        name="encode",
    )(starts, logits, padded_ids, idf_pad)


def pad_features(values):
    lead = values.shape[:-1]
    split = values.reshape(lead + (STATES, COLS))
    return jnp.pad(split, ((0, 0),) * (len(lead) + 1) + ((0, LANES - COLS),))


def on_device(logits, entry_ids, query_counts, idf_weights):
    db_count = lax.axis_size("db")
    query_count = lax.axis_size("query")
    chips = query_count // CORES
    chip = lax.axis_index("query") // CORES
    share_rows = E_DEV // query_count
    most_rows = share_rows + 3 * share_rows // 4
    rows = align_up(most_rows + db_count, max(16, db_count))

    scaled = query_counts.astype(jnp.float32) * idf_weights
    query_rows = (
        scaled / jnp.sqrt(jnp.sum(scaled * scaled, axis=-1, keepdims=True) + EPSILON)
    ).astype(jnp.bfloat16)
    query_rows = pad_features(query_rows).reshape(query_counts.shape[0], STATES * LANES)
    segment = lax.all_gather(query_rows, "db", axis=0, tiled=True)
    swap = [(q, q ^ 1) for q in range(query_count)]
    other = lax.ppermute(segment, "query", swap)

    idf_pad = pad_features(idf_weights)
    tables = []
    for step in range(chips):
        if step == 0:
            shard, shard_ids = logits, entry_ids
        else:
            ring = [(q, (q + CORES * step) % query_count) for q in range(query_count)]
            shard = lax.ppermute(logits, "query", ring)
            shard_ids = lax.ppermute(entry_ids, "query", ring)
        tables.append(encode(shard, shard_ids, idf_pad, rows, db_count))

    def best(table, queries):
        scores = lax.dot_general(
            table, queries, (((1,), (1,)), ((), ())), preferred_element_type=jnp.float32
        )
        return jnp.max(scores.reshape(rows // db_count, db_count, queries.shape[0]), axis=0)

    def halves(queries):
        parts = [best(table, queries) for table in tables]
        places = [(chip - step) % chips * HALVES // chips for step in range(chips)]
        return jnp.stack(
            [
                functools.reduce(
                    jnp.maximum,
                    [jnp.where(place == half, part, -jnp.inf) for place, part in zip(places, parts)],
                )
                for half in range(HALVES)
            ],
            axis=1,
        )

    mine = jnp.maximum(halves(segment), lax.ppermute(halves(other), "query", swap))
    arrived = lax.all_to_all(mine, "db", split_axis=0, concat_axis=0, tiled=True)
    return jnp.max(arrived, axis=0)


def solution(mesh):
    placed = (P(None, ("query", "db")), P(("query", "db")), P(("query", "db"), None), P())
    return jax.shard_map(
        on_device, mesh=mesh, in_specs=placed, out_specs=P("db", "query"), check_vma=False
    )
```

```python
import functools
import math

import jax
import jax.numpy as jnp
from jax import lax
from jax.experimental import pallas as pl
from jax.experimental.pallas import tpu as pltpu
from jax.sharding import PartitionSpec as P

STATES = 20
OFFSETS = 6
COLS = STATES * OFFSETS
LANES = 128
BR = 256
WINDOW = 16
E_DEV = 1024
HALVES = 2
CORES = 2
OUTER = 4
EPSILON = 1e-06
HALO = 128


def align_up(value, unit):
    return -(-value // unit) * unit


def encode_kernel(
    residues,
    rows,
    chunk,
    db_count,
    marks_ref,
    logits_ref,
    own_ref,
    idf_ref,
    out_ref,
    probs,
    partner,
    table,
    ids,
):
    first_id = marks_ref[0]
    origin = first_id - lax.rem(first_id, db_count)
    ids[:, :residues] = own_ref[...]
    ids[:, residues:] = jnp.full((1, HALO), -1, jnp.int32)
    table[...] = jnp.zeros_like(table)
    partner[COLS:, :] = jnp.zeros((LANES - COLS, chunk), jnp.float32)
    probs[:, residues:] = jnp.zeros((STATES, HALO), jnp.float32)

    def soften(step, carry):
        cols = pl.ds(pl.multiple_of(step * chunk, chunk), chunk)
        values = logits_ref[:, cols].astype(jnp.float32)
        values = jnp.exp(values - jnp.max(values, axis=0, keepdims=True))
        values = values / jnp.sum(values, axis=0, keepdims=True)
        probs[:, cols] = values.astype(jnp.bfloat16).astype(jnp.float32)
        return carry

    lax.fori_loop(0, residues // chunk, soften, 0)
    slots = lax.broadcasted_iota(jnp.int32, (WINDOW, BR), 0)

    def add_chunk(step, carry):
        first = pl.multiple_of(step * chunk, chunk)
        wide = pl.ds(first, chunk + HALO)
        prob_slab = probs[:, wide]
        id_slab = ids[:, wide]
        own_ids = id_slab[:, :chunk]
        for offset in range(OFFSETS):
            shift = chunk + HALO - offset - 1
            moved = pltpu.roll(prob_slab, shift, 1)[:, :chunk]
            moved_ids = pltpu.roll(id_slab, shift, 1)[:, :chunk]
            partner[offset * STATES : (offset + 1) * STATES, :] = jnp.where(
                moved_ids == own_ids, moved, 0.0
            )
        for block in range(chunk // BR):
            here = slice(block * BR, (block + 1) * BR)
            start = (marks_ref[first + block * BR] - origin) // 8 * 8
            base = pl.multiple_of(jnp.clip(start, 0, rows - WINDOW), 8)
            onehot = (own_ids[:, here] - (origin + base)) == slots
            spread = jnp.concatenate(
                [
                    jnp.where(onehot, prob_slab[a : a + 1, here], 0.0).astype(jnp.bfloat16)
                    for a in range(STATES)
                ],
                axis=0,
            )
            sums = lax.dot_general(
                spread,
                partner[:, here].astype(jnp.bfloat16),
                (((1,), (1,)), ((), ())),
                preferred_element_type=jnp.float32,
            )
            for a in range(STATES):
                table[a, pl.ds(base, WINDOW), :] += sums[a * WINDOW : (a + 1) * WINDOW]
        return carry

    lax.fori_loop(0, residues // chunk, add_chunk, 0)

    def finish(step, carry):
        part = pl.ds(pl.multiple_of(step * 16, 16), 16)
        total = jnp.zeros((16, LANES), jnp.float32)
        for a in range(STATES):
            scaled = table[a, part, :] * idf_ref[a : a + 1, :]
            total += scaled * scaled
        norm = jnp.sqrt(jnp.sum(total, axis=1, keepdims=True) + EPSILON)
        for a in range(STATES):
            scaled = table[a, part, :] * idf_ref[a : a + 1, :]
            out_ref[part, a * LANES : (a + 1) * LANES] = (scaled / norm).astype(jnp.bfloat16)
        return carry

    lax.fori_loop(0, rows // 16, finish, 0)


def encode(logits, entry_ids, idf_pad, rows, db_count):
    residues = logits.shape[1]
    chunk = min(2048, residues)
    vmem = pl.BlockSpec(memory_space=pltpu.VMEM)
    return pl.pallas_call(
        functools.partial(encode_kernel, residues, rows, chunk, db_count),
        out_shape=jax.ShapeDtypeStruct((rows, STATES * LANES), jnp.bfloat16),
        in_specs=[pl.BlockSpec(memory_space=pltpu.SMEM), vmem, vmem, vmem],
        out_specs=vmem,
        scratch_shapes=[
            pltpu.VMEM((STATES, residues + HALO), jnp.float32),
            pltpu.VMEM((LANES, chunk), jnp.float32),
            pltpu.VMEM((STATES, rows, LANES), jnp.float32),
            pltpu.VMEM((1, residues + HALO), jnp.int32),
        ],
        cost_estimate=pl.CostEstimate(
            flops=2 * residues * STATES * WINDOW * LANES,
            bytes_accessed=residues * 44 + rows * STATES * LANES * 2,
            transcendentals=residues * STATES,
        ),
        compiler_params=pltpu.CompilerParams(vmem_limit_bytes=32 * 1024 * 1024),
        name="encode",
    )(entry_ids, logits, entry_ids.reshape(1, residues), idf_pad)


def pad_features(values):
    lead = values.shape[:-1]
    split = values.reshape(lead + (STATES, COLS))
    return jnp.pad(split, ((0, 0),) * (len(lead) + 1) + ((0, LANES - COLS),))


def on_device(logits, entry_ids, query_counts, idf_weights):
    db_count = lax.axis_size("db")
    query_count = lax.axis_size("query")
    chips = query_count // CORES
    chip = lax.axis_index("query") // CORES
    share_rows = E_DEV // query_count
    most_rows = share_rows + 3 * share_rows // 4
    rows = align_up(most_rows + db_count, max(16, db_count))

    scaled = query_counts.astype(jnp.float32) * idf_weights
    query_rows = (
        scaled / jnp.sqrt(jnp.sum(scaled * scaled, axis=-1, keepdims=True) + EPSILON)
    ).astype(jnp.bfloat16)
    query_rows = pad_features(query_rows).reshape(query_counts.shape[0], STATES * LANES)
    outer = math.gcd(db_count, OUTER)
    inner = db_count // outer
    place = lax.axis_index("db")
    swap = [(q, q ^ 1) for q in range(query_count)]
    outer_ring = [(d, (d + inner) % db_count) for d in range(db_count)]
    inner_ring = [(d, d // inner * inner + (d + 1) % inner) for d in range(db_count)]

    shards = [(logits, entry_ids)]
    for step in range(1, chips):
        ring = [(q, (q + CORES * step) % query_count) for q in range(query_count)]
        shards.append(
            (lax.ppermute(logits, "query", ring), lax.ppermute(entry_ids, "query", ring))
        )

    groups = []
    lead = query_rows
    for far in range(outer):
        if far > 0:
            lead = lax.ppermute(lead, "db", outer_ring)
        group = [lead]
        for _ in range(1, inner):
            group.append(lax.ppermute(group[-1], "db", inner_ring))
        groups.append(group)

    idf_pad = pad_features(idf_weights)
    tables = []
    for step, (shard, shard_ids) in enumerate(shards):
        table = encode(shard, shard_ids, idf_pad, rows, db_count)
        source = (chip - step) % chips * HALVES // chips
        tables += [(source, table), (source, lax.ppermute(table, "query", swap))]

    def best(table, queries):
        scores = lax.dot_general(
            table, queries, (((1,), (1,)), ((), ())), preferred_element_type=jnp.float32
        )
        return jnp.max(scores.reshape(rows // db_count, db_count, queries.shape[0]), axis=0)

    def halves(queries):
        parts = [(source, best(table, queries)) for source, table in tables]
        return jnp.stack(
            [
                functools.reduce(
                    jnp.maximum,
                    [jnp.where(source == half, part, -jnp.inf) for source, part in parts],
                )
                for half in range(HALVES)
            ],
            axis=1,
        )

    share = query_counts.shape[0]
    found = [
        halves(jnp.concatenate(group, axis=0)).reshape(db_count, HALVES, inner, share)
        for group in groups
    ]
    found = jnp.stack(found, axis=2).reshape(db_count, HALVES, db_count, share)
    targets = jnp.arange(db_count, dtype=jnp.int32)
    order = (place // inner - targets // inner) % outer * inner + (place - targets) % inner
    mine = jnp.take(found, order, axis=2).reshape(db_count, HALVES, db_count * share)
    arrived = lax.all_to_all(mine, "db", split_axis=0, concat_axis=0, tiled=True)
    return jnp.max(arrived, axis=0)


def solution(mesh):
    placed = (P(None, ("query", "db")), P(("query", "db")), P(("query", "db"), None), P())
    return jax.shard_map(
        on_device, mesh=mesh, in_specs=placed, out_specs=P("db", "query"), check_vma=False
    )
```

```python
import functools
import math

import jax
import jax.numpy as jnp
from jax import lax
from jax.experimental import pallas as pl
from jax.experimental.pallas import tpu as pltpu
from jax.sharding import PartitionSpec as P

STATES = 20
OFFSETS = 6
COLS = STATES * OFFSETS
LANES = 128
BR = 256
WINDOW = 16
E_DEV = 1024
HALVES = 2
CORES = 2
OUTER = 4
EPSILON = 1e-06
HALO = 128


def align_up(value, unit):
    return -(-value // unit) * unit


def encode_kernel(
    residues,
    rows,
    chunk,
    db_count,
    marks_ref,
    logits_ref,
    own_ref,
    idf_ref,
    out_ref,
    probs,
    partner,
    table,
    ids,
):
    first_id = marks_ref[0]
    origin = first_id - lax.rem(first_id, db_count)
    ids[:, :residues] = own_ref[...]
    ids[:, residues:] = jnp.full((1, HALO), -1, jnp.int32)
    table[...] = jnp.zeros_like(table)
    partner[COLS:, :] = jnp.zeros((LANES - COLS, chunk), jnp.float32)
    probs[:, residues:] = jnp.zeros((STATES, HALO), jnp.float32)

    def soften(step, carry):
        cols = pl.ds(pl.multiple_of(step * chunk, chunk), chunk)
        values = logits_ref[:, cols].astype(jnp.float32)
        values = jnp.exp(values - jnp.max(values, axis=0, keepdims=True))
        values = values / jnp.sum(values, axis=0, keepdims=True)
        probs[:, cols] = values.astype(jnp.bfloat16).astype(jnp.float32)
        return carry

    lax.fori_loop(0, residues // chunk, soften, 0)
    slots = lax.broadcasted_iota(jnp.int32, (WINDOW, BR), 0)

    def add_chunk(step, carry):
        first = pl.multiple_of(step * chunk, chunk)
        wide = pl.ds(first, chunk + HALO)
        prob_slab = probs[:, wide]
        id_slab = ids[:, wide]
        own_ids = id_slab[:, :chunk]
        for offset in range(OFFSETS):
            shift = chunk + HALO - offset - 1
            moved = pltpu.roll(prob_slab, shift, 1)[:, :chunk]
            moved_ids = pltpu.roll(id_slab, shift, 1)[:, :chunk]
            partner[offset * STATES : (offset + 1) * STATES, :] = jnp.where(
                moved_ids == own_ids, moved, 0.0
            )
        for block in range(chunk // BR):
            here = slice(block * BR, (block + 1) * BR)
            start = (marks_ref[step * (chunk // BR) + block] - origin) // 8 * 8
            base = pl.multiple_of(jnp.clip(start, 0, rows - WINDOW), 8)
            onehot = (own_ids[:, here] - (origin + base)) == slots
            spread = jnp.concatenate(
                [
                    jnp.where(onehot, prob_slab[a : a + 1, here], 0.0).astype(jnp.bfloat16)
                    for a in range(STATES)
                ],
                axis=0,
            )
            sums = lax.dot_general(
                spread,
                partner[:, here].astype(jnp.bfloat16),
                (((1,), (1,)), ((), ())),
                preferred_element_type=jnp.float32,
            )
            for a in range(STATES):
                table[a, pl.ds(base, WINDOW), :] += sums[a * WINDOW : (a + 1) * WINDOW]
        return carry

    lax.fori_loop(0, residues // chunk, add_chunk, 0)

    def finish(step, carry):
        part = pl.ds(pl.multiple_of(step * 16, 16), 16)
        total = jnp.zeros((16, LANES), jnp.float32)
        for a in range(STATES):
            scaled = table[a, part, :] * idf_ref[a : a + 1, :]
            total += scaled * scaled
        norm = jnp.sqrt(jnp.sum(total, axis=1, keepdims=True) + EPSILON)
        for a in range(STATES):
            scaled = table[a, part, :] * idf_ref[a : a + 1, :]
            out_ref[part, a * LANES : (a + 1) * LANES] = (scaled / norm).astype(jnp.bfloat16)
        return carry

    lax.fori_loop(0, rows // 16, finish, 0)


def encode(logits, entry_ids, marks, idf_pad, rows, db_count):
    residues = logits.shape[1]
    chunk = min(2048, residues)
    vmem = pl.BlockSpec(memory_space=pltpu.VMEM)
    return pl.pallas_call(
        functools.partial(encode_kernel, residues, rows, chunk, db_count),
        out_shape=jax.ShapeDtypeStruct((rows, STATES * LANES), jnp.bfloat16),
        in_specs=[pl.BlockSpec(memory_space=pltpu.SMEM), vmem, vmem, vmem],
        out_specs=vmem,
        scratch_shapes=[
            pltpu.VMEM((STATES, residues + HALO), jnp.float32),
            pltpu.VMEM((LANES, chunk), jnp.float32),
            pltpu.VMEM((STATES, rows, LANES), jnp.float32),
            pltpu.VMEM((1, residues + HALO), jnp.int32),
        ],
        cost_estimate=pl.CostEstimate(
            flops=16 * residues * STATES * WINDOW * LANES,
            bytes_accessed=residues * 44 + rows * STATES * LANES * 2,
            transcendentals=residues * STATES,
        ),
        compiler_params=pltpu.CompilerParams(vmem_limit_bytes=32 * 1024 * 1024),
        name="encode",
    )(marks, logits, entry_ids.reshape(1, residues), idf_pad)


def pad_features(values):
    lead = values.shape[:-1]
    split = values.reshape(lead + (STATES, COLS))
    return jnp.pad(split, ((0, 0),) * (len(lead) + 1) + ((0, LANES - COLS),))


def on_device(logits, entry_ids, query_counts, idf_weights):
    db_count = lax.axis_size("db")
    query_count = lax.axis_size("query")
    chips = query_count // CORES
    chip = lax.axis_index("query") // CORES
    share_rows = E_DEV // query_count
    most_rows = share_rows + 3 * share_rows // 4
    rows = align_up(most_rows + db_count, max(16, db_count))

    scaled = query_counts.astype(jnp.float32) * idf_weights
    query_rows = (
        scaled / jnp.sqrt(jnp.sum(scaled * scaled, axis=-1, keepdims=True) + EPSILON)
    ).astype(jnp.bfloat16)
    query_rows = pad_features(query_rows).reshape(query_counts.shape[0], STATES * LANES)
    outer = math.gcd(db_count, OUTER)
    inner = db_count // outer
    place = lax.axis_index("db")
    swap = [(q, q ^ 1) for q in range(query_count)]
    outer_ring = [(d, (d + inner) % db_count) for d in range(db_count)]
    inner_ring = [(d, d // inner * inner + (d + 1) % inner) for d in range(db_count)]

    marks = entry_ids[::BR]
    shards = [(logits, entry_ids, marks)]
    for step in range(1, chips):
        ring = [(q, (q + CORES * step) % query_count) for q in range(query_count)]
        shards.append(tuple(lax.ppermute(part, "query", ring) for part in shards[0]))

    groups = []
    lead = query_rows
    for far in range(outer):
        if far > 0:
            lead = lax.ppermute(lead, "db", outer_ring)
        if far == outer - 2:
            lead, shards[1:] = lax.optimization_barrier((lead, shards[1:]))
        group = [lead]
        for _ in range(1, inner):
            group.append(lax.ppermute(group[-1], "db", inner_ring))
        groups.append(group)

    idf_pad = pad_features(idf_weights)
    tables = []
    for step, shard in enumerate(shards):
        table = encode(*shard, idf_pad, rows, db_count)
        source = (chip - step) % chips * HALVES // chips
        tables += [(source, table), (source, lax.ppermute(table, "query", swap))]

    def best(table, queries):
        scores = lax.dot_general(
            table, queries, (((1,), (1,)), ((), ())), preferred_element_type=jnp.float32
        )
        return jnp.max(scores.reshape(rows // db_count, db_count, queries.shape[0]), axis=0)

    def halves(queries):
        parts = [(source, best(table, queries)) for source, table in tables]
        return jnp.stack(
            [
                functools.reduce(
                    jnp.maximum,
                    [jnp.where(source == half, part, -jnp.inf) for source, part in parts],
                )
                for half in range(HALVES)
            ],
            axis=1,
        )

    share = query_counts.shape[0]
    found = [
        halves(jnp.concatenate(group, axis=0)).reshape(db_count, HALVES, inner, share)
        for group in groups
    ]
    found = jnp.stack(found, axis=2).reshape(db_count, HALVES, db_count, share)
    targets = jnp.arange(db_count, dtype=jnp.int32)
    order = (place // inner - targets // inner) % outer * inner + (place - targets) % inner
    mine = jnp.take(found, order, axis=2).reshape(db_count, HALVES, db_count * share)
    arrived = lax.all_to_all(mine, "db", split_axis=0, concat_axis=0, tiled=True)
    return jnp.max(arrived, axis=0)


def solution(mesh):
    placed = (P(None, ("query", "db")), P(("query", "db")), P(("query", "db"), None), P())
    return jax.shard_map(
        on_device, mesh=mesh, in_specs=placed, out_specs=P("db", "query"), check_vma=False
    )
```

```python
import functools
import math

import jax
import jax.numpy as jnp
from jax import lax
from jax.experimental import pallas as pl
from jax.experimental.pallas import tpu as pltpu
from jax.sharding import PartitionSpec as P

STATES = 20
OFFSETS = 6
COLS = STATES * OFFSETS
LANES = 128
BR = 256
WINDOW = 16
E_DEV = 1024
HALVES = 2
CORES = 2
OUTER = 4
EPSILON = 1e-06
HALO = 128


def align_up(value, unit):
    return -(-value // unit) * unit


def encode_kernel(
    residues,
    rows,
    chunk,
    db_count,
    marks_ref,
    logits_ref,
    own_ref,
    idf_ref,
    out_ref,
    probs,
    partner,
    table,
    ids,
):
    first_id = marks_ref[0]
    origin = first_id - lax.rem(first_id, db_count)
    ids[:, :residues] = own_ref[...]
    ids[:, residues:] = jnp.full((1, HALO), -1, jnp.int32)
    table[...] = jnp.zeros_like(table)
    partner[COLS:, :] = jnp.zeros((LANES - COLS, chunk), jnp.float32)
    probs[:, residues:] = jnp.zeros((STATES, HALO), jnp.float32)

    def soften(step, carry):
        cols = pl.ds(pl.multiple_of(step * chunk, chunk), chunk)
        values = logits_ref[:, cols].astype(jnp.float32)
        values = jnp.exp(values - jnp.max(values, axis=0, keepdims=True))
        values = values / jnp.sum(values, axis=0, keepdims=True)
        probs[:, cols] = values.astype(jnp.bfloat16).astype(jnp.float32)
        return carry

    lax.fori_loop(0, residues // chunk, soften, 0)
    slots = lax.broadcasted_iota(jnp.int32, (WINDOW, BR), 0)

    def add_chunk(step, carry):
        first = pl.multiple_of(step * chunk, chunk)
        wide = pl.ds(first, chunk + HALO)
        prob_slab = probs[:, wide]
        id_slab = ids[:, wide]
        own_ids = id_slab[:, :chunk]
        for offset in range(OFFSETS):
            shift = chunk + HALO - offset - 1
            moved = pltpu.roll(prob_slab, shift, 1)[:, :chunk]
            moved_ids = pltpu.roll(id_slab, shift, 1)[:, :chunk]
            partner[offset * STATES : (offset + 1) * STATES, :] = jnp.where(
                moved_ids == own_ids, moved, 0.0
            )
        for block in range(chunk // BR):
            here = slice(block * BR, (block + 1) * BR)
            start = (marks_ref[step * (chunk // BR) + block] - origin) // 8 * 8
            base = pl.multiple_of(jnp.clip(start, 0, rows - WINDOW), 8)
            onehot = (own_ids[:, here] - (origin + base)) == slots
            spread = jnp.concatenate(
                [
                    jnp.where(onehot, prob_slab[a : a + 1, here], 0.0).astype(jnp.bfloat16)
                    for a in range(STATES)
                ],
                axis=0,
            )
            sums = lax.dot_general(
                spread,
                partner[:, here].astype(jnp.bfloat16),
                (((1,), (1,)), ((), ())),
                preferred_element_type=jnp.float32,
            )
            for a in range(STATES):
                table[a, pl.ds(base, WINDOW), :] += sums[a * WINDOW : (a + 1) * WINDOW]
        return carry

    lax.fori_loop(0, residues // chunk, add_chunk, 0)

    def finish(step, carry):
        part = pl.ds(pl.multiple_of(step * 16, 16), 16)
        total = jnp.zeros((16, LANES), jnp.float32)
        for a in range(STATES):
            scaled = table[a, part, :] * idf_ref[a : a + 1, :]
            total += scaled * scaled
        norm = jnp.sqrt(jnp.sum(total, axis=1, keepdims=True) + EPSILON)
        for a in range(STATES):
            scaled = table[a, part, :] * idf_ref[a : a + 1, :]
            out_ref[part, a * LANES : (a + 1) * LANES] = (scaled / norm).astype(jnp.bfloat16)
        return carry

    lax.fori_loop(0, rows // 16, finish, 0)


def encode(logits, entry_ids, marks, idf_pad, rows, db_count):
    residues = logits.shape[1]
    chunk = min(2048, residues)
    vmem = pl.BlockSpec(memory_space=pltpu.VMEM)
    return pl.pallas_call(
        functools.partial(encode_kernel, residues, rows, chunk, db_count),
        out_shape=jax.ShapeDtypeStruct((rows, STATES * LANES), jnp.bfloat16),
        in_specs=[pl.BlockSpec(memory_space=pltpu.SMEM), vmem, vmem, vmem],
        out_specs=vmem,
        scratch_shapes=[
            pltpu.VMEM((STATES, residues + HALO), jnp.float32),
            pltpu.VMEM((LANES, chunk), jnp.float32),
            pltpu.VMEM((STATES, rows, LANES), jnp.float32),
            pltpu.VMEM((1, residues + HALO), jnp.int32),
        ],
        cost_estimate=pl.CostEstimate(
            flops=16 * residues * STATES * WINDOW * LANES,
            bytes_accessed=residues * 44 + rows * STATES * LANES * 2,
            transcendentals=residues * STATES,
        ),
        compiler_params=pltpu.CompilerParams(vmem_limit_bytes=32 * 1024 * 1024),
        name="encode",
    )(marks, logits, entry_ids.reshape(1, residues), idf_pad)


def pad_features(values):
    lead = values.shape[:-1]
    split = values.reshape(lead + (STATES, COLS))
    return jnp.pad(split, ((0, 0),) * (len(lead) + 1) + ((0, LANES - COLS),))


def on_device(logits, entry_ids, query_counts, idf_weights):
    db_count = lax.axis_size("db")
    query_count = lax.axis_size("query")
    chips = query_count // CORES
    chip = lax.axis_index("query") // CORES
    share_rows = E_DEV // query_count
    most_rows = share_rows + 3 * share_rows // 4
    rows = align_up(most_rows + db_count, max(16, db_count))

    scaled = query_counts.astype(jnp.float32) * idf_weights
    query_rows = (
        scaled / jnp.sqrt(jnp.sum(scaled * scaled, axis=-1, keepdims=True) + EPSILON)
    ).astype(jnp.bfloat16)
    query_rows = pad_features(query_rows).reshape(query_counts.shape[0], STATES * LANES)
    outer = math.gcd(db_count, OUTER)
    inner = db_count // outer
    place = lax.axis_index("db")
    swap = [(q, q ^ 1) for q in range(query_count)]
    outer_ring = [(d, (d + inner) % db_count) for d in range(db_count)]
    outer_back = [(d, (d - inner) % db_count) for d in range(db_count)]
    inner_ring = [(d, d // inner * inner + (d + 1) % inner) for d in range(db_count)]

    marks = entry_ids[::BR]
    shards = [(logits, entry_ids, marks)]
    for step in range(1, chips):
        ring = [(q, (q + CORES * step) % query_count) for q in range(query_count)]
        shards.append(tuple(lax.ppermute(part, "query", ring) for part in shards[0]))

    groups = []
    lead = query_rows
    for far in range(outer):
        if far == outer - 1 and far > 1:
            lead = lax.ppermute(query_rows, "db", outer_back)
        elif far > 0:
            lead = lax.ppermute(lead, "db", outer_ring)
        if far == outer - 2:
            lead, shards[1:] = lax.optimization_barrier((lead, shards[1:]))
        group = [lead]
        for _ in range(1, inner):
            group.append(lax.ppermute(group[-1], "db", inner_ring))
        groups.append(group)

    idf_pad = pad_features(idf_weights)
    tables = []
    for step, shard in enumerate(shards):
        table = encode(*shard, idf_pad, rows, db_count)
        source = (chip - step) % chips * HALVES // chips
        tables += [(source, table), (source, lax.ppermute(table, "query", swap))]

    def best(table, queries):
        scores = lax.dot_general(
            table, queries, (((1,), (1,)), ((), ())), preferred_element_type=jnp.float32
        )
        return jnp.max(scores.reshape(rows // db_count, db_count, queries.shape[0]), axis=0)

    def halves(queries):
        parts = [(source, best(table, queries)) for source, table in tables]
        return jnp.stack(
            [
                functools.reduce(
                    jnp.maximum,
                    [jnp.where(source == half, part, -jnp.inf) for source, part in parts],
                )
                for half in range(HALVES)
            ],
            axis=1,
        )

    share = query_counts.shape[0]
    found = [
        halves(jnp.concatenate(group, axis=0)).reshape(db_count, HALVES, inner, share)
        for group in groups
    ]
    found = jnp.stack(found, axis=2).reshape(db_count, HALVES, db_count, share)
    targets = jnp.arange(db_count, dtype=jnp.int32)
    order = (place // inner - targets // inner) % outer * inner + (place - targets) % inner
    mine = jnp.take(found, order, axis=2).reshape(db_count, HALVES, db_count * share)
    arrived = lax.all_to_all(mine, "db", split_axis=0, concat_axis=0, tiled=True)
    return jnp.max(arrived, axis=0)


def solution(mesh):
    placed = (P(None, ("query", "db")), P(("query", "db")), P(("query", "db"), None), P())
    return jax.shard_map(
        on_device, mesh=mesh, in_specs=placed, out_specs=P("db", "query"), check_vma=False
    )
```

```python
import functools
import math

import jax
import jax.numpy as jnp
from jax import lax
from jax.experimental import pallas as pl
from jax.experimental.pallas import tpu as pltpu
from jax.sharding import PartitionSpec as P

STATES = 20
OFFSETS = 6
COLS = STATES * OFFSETS
LANES = 128
BR = 256
WINDOW = 16
E_DEV = 1024
HALVES = 2
CORES = 2
OUTER = 4
EPSILON = 1e-06
HALO = 128


def align_up(value, unit):
    return -(-value // unit) * unit


def encode_kernel(
    residues,
    rows,
    chunk,
    db_count,
    marks_ref,
    logits_ref,
    own_ref,
    idf_ref,
    out_ref,
    probs,
    partner,
    table,
    ids,
):
    first_id = marks_ref[0]
    origin = first_id - lax.rem(first_id, db_count)
    ids[:, :residues] = own_ref[...]
    ids[:, residues:] = jnp.full((1, HALO), -1, jnp.int32)
    table[...] = jnp.zeros_like(table)
    partner[COLS:, :] = jnp.zeros((LANES - COLS, chunk), jnp.float32)
    probs[:, residues:] = jnp.zeros((STATES, HALO), jnp.float32)

    def soften(step, carry):
        cols = pl.ds(pl.multiple_of(step * chunk, chunk), chunk)
        values = logits_ref[:, cols].astype(jnp.float32)
        values = jnp.exp(values - jnp.max(values, axis=0, keepdims=True))
        values = values / jnp.sum(values, axis=0, keepdims=True)
        probs[:, cols] = values.astype(jnp.bfloat16).astype(jnp.float32)
        return carry

    lax.fori_loop(0, residues // chunk, soften, 0)
    slots = lax.broadcasted_iota(jnp.int32, (WINDOW, BR), 0)

    def add_chunk(step, carry):
        first = pl.multiple_of(step * chunk, chunk)
        wide = pl.ds(first, chunk + HALO)
        prob_slab = probs[:, wide]
        id_slab = ids[:, wide]
        own_ids = id_slab[:, :chunk]
        for offset in range(OFFSETS):
            shift = chunk + HALO - offset - 1
            moved = pltpu.roll(prob_slab, shift, 1)[:, :chunk]
            moved_ids = pltpu.roll(id_slab, shift, 1)[:, :chunk]
            partner[offset * STATES : (offset + 1) * STATES, :] = jnp.where(
                moved_ids == own_ids, moved, 0.0
            )
        for block in range(chunk // BR):
            here = slice(block * BR, (block + 1) * BR)
            start = (marks_ref[step * (chunk // BR) + block] - origin) // 8 * 8
            base = pl.multiple_of(jnp.clip(start, 0, rows - WINDOW), 8)
            onehot = (own_ids[:, here] - (origin + base)) == slots
            spread = jnp.concatenate(
                [
                    jnp.where(onehot, prob_slab[a : a + 1, here], 0.0).astype(jnp.bfloat16)
                    for a in range(STATES)
                ],
                axis=0,
            )
            sums = lax.dot_general(
                spread,
                partner[:, here].astype(jnp.bfloat16),
                (((1,), (1,)), ((), ())),
                preferred_element_type=jnp.float32,
            )
            for a in range(STATES):
                table[a, pl.ds(base, WINDOW), :] += sums[a * WINDOW : (a + 1) * WINDOW]
        return carry

    lax.fori_loop(0, residues // chunk, add_chunk, 0)

    def finish(step, carry):
        part = pl.ds(pl.multiple_of(step * 16, 16), 16)
        total = jnp.zeros((16, LANES), jnp.float32)
        for a in range(STATES):
            scaled = table[a, part, :] * idf_ref[a : a + 1, :]
            total += scaled * scaled
        norm = jnp.sqrt(jnp.sum(total, axis=1, keepdims=True) + EPSILON)
        for a in range(STATES):
            scaled = table[a, part, :] * idf_ref[a : a + 1, :]
            out_ref[part, a * LANES : (a + 1) * LANES] = (scaled / norm).astype(jnp.bfloat16)
        return carry

    lax.fori_loop(0, rows // 16, finish, 0)


def encode(logits, entry_ids, marks, idf_pad, rows, db_count):
    residues = logits.shape[1]
    chunk = min(2048, residues)
    vmem = pl.BlockSpec(memory_space=pltpu.VMEM)
    return pl.pallas_call(
        functools.partial(encode_kernel, residues, rows, chunk, db_count),
        out_shape=jax.ShapeDtypeStruct((rows, STATES * LANES), jnp.bfloat16),
        in_specs=[pl.BlockSpec(memory_space=pltpu.SMEM), vmem, vmem, vmem],
        out_specs=vmem,
        scratch_shapes=[
            pltpu.VMEM((STATES, residues + HALO), jnp.float32),
            pltpu.VMEM((LANES, chunk), jnp.float32),
            pltpu.VMEM((STATES, rows, LANES), jnp.float32),
            pltpu.VMEM((1, residues + HALO), jnp.int32),
        ],
        cost_estimate=pl.CostEstimate(
            flops=16 * residues * STATES * WINDOW * LANES,
            bytes_accessed=residues * 44 + rows * STATES * LANES * 2,
            transcendentals=residues * STATES,
        ),
        compiler_params=pltpu.CompilerParams(vmem_limit_bytes=32 * 1024 * 1024),
        name="encode",
    )(marks, logits, entry_ids.reshape(1, residues), idf_pad)


def pad_features(values):
    lead = values.shape[:-1]
    split = values.reshape(lead + (STATES, COLS))
    return jnp.pad(split, ((0, 0),) * (len(lead) + 1) + ((0, LANES - COLS),))


def on_device(logits, entry_ids, query_counts, idf_weights):
    db_count = lax.axis_size("db")
    query_count = lax.axis_size("query")
    chips = query_count // CORES
    chip = lax.axis_index("query") // CORES
    share_rows = E_DEV // query_count
    most_rows = share_rows + 3 * share_rows // 4
    rows = align_up(most_rows + db_count, max(16, db_count))

    scaled = query_counts.astype(jnp.float32) * idf_weights
    query_rows = (
        scaled / jnp.sqrt(jnp.sum(scaled * scaled, axis=-1, keepdims=True) + EPSILON)
    ).astype(jnp.bfloat16)
    query_rows = pad_features(query_rows).reshape(query_counts.shape[0], STATES * LANES)
    outer = math.gcd(db_count, OUTER)
    inner = db_count // outer
    place = lax.axis_index("db")
    swap = [(q, q ^ 1) for q in range(query_count)]
    outer_ring = [(d, (d + inner) % db_count) for d in range(db_count)]
    outer_back = [(d, (d - inner) % db_count) for d in range(db_count)]
    inner_ring = [(d, d // inner * inner + (d + 1) % inner) for d in range(db_count)]

    marks = entry_ids[::BR]
    shards = [(logits, entry_ids, marks)]
    for step in range(1, chips):
        ring = [(q, (q + CORES * step) % query_count) for q in range(query_count)]
        shards.append(tuple(lax.ppermute(part, "query", ring) for part in shards[0]))

    groups = []
    lead = query_rows
    for far in range(outer):
        if far == outer - 1 and far > 1:
            lead = lax.ppermute(query_rows, "db", outer_back)
        elif far > 0:
            lead = lax.ppermute(lead, "db", outer_ring)
        group = [lead]
        for _ in range(1, inner):
            group.append(lax.ppermute(group[-1], "db", inner_ring))
        groups.append(group)

    idf_pad = pad_features(idf_weights)
    tables = []
    for step, shard in enumerate(shards):
        table = encode(*shard, idf_pad, rows, db_count)
        source = (chip - step) % chips * HALVES // chips
        tables += [(source, table), (source, lax.ppermute(table, "query", swap))]

    def best(table, queries):
        scores = lax.dot_general(
            table, queries, (((1,), (1,)), ((), ())), preferred_element_type=jnp.float32
        )
        return jnp.max(scores.reshape(rows // db_count, db_count, queries.shape[0]), axis=0)

    def halves(queries):
        parts = [(source, best(table, queries)) for source, table in tables]
        return jnp.stack(
            [
                functools.reduce(
                    jnp.maximum,
                    [jnp.where(source == half, part, -jnp.inf) for source, part in parts],
                )
                for half in range(HALVES)
            ],
            axis=1,
        )

    share = query_counts.shape[0]
    found = [
        halves(jnp.concatenate(group, axis=0)).reshape(db_count, HALVES, inner, share)
        for group in groups
    ]
    found = jnp.stack(found, axis=2).reshape(db_count, HALVES, db_count, share)
    targets = jnp.arange(db_count, dtype=jnp.int32)
    order = (place // inner - targets // inner) % outer * inner + (place - targets) % inner
    mine = jnp.take(found, order, axis=2).reshape(db_count, HALVES, db_count * share)
    arrived = lax.all_to_all(mine, "db", split_axis=0, concat_axis=0, tiled=True)
    return jnp.max(arrived, axis=0)


def solution(mesh):
    placed = (P(None, ("query", "db")), P(("query", "db")), P(("query", "db"), None), P())
    return jax.shard_map(
        on_device, mesh=mesh, in_specs=placed, out_specs=P("db", "query"), check_vma=False
    )
```
